32 devices in a mesh: freq: 2 (over x), tile: 16 (over z, y, core).
Axes of the slice: x: 2, y: 2, z: 4, core: 2. Of those that a mesh axis runs over, the one named last changes fastest.
Arguments:
- left_basis: bfloat16 [4, 8192, 2, 1536], P('freq', 'tile'), may hold values from -0.078125 to 0.078125
- right_basis: bfloat16 [4, 8192, 2, 1536], P('freq', 'tile'), may hold values from -0.25 to 0.25
- start_model: float32 [4, 8192, 128], P('freq', 'tile'), may hold values from -3 to 3
- recorded: float32 [4, 8192, 128], P('freq', 'tile'), may hold values from -6 to 6
- tile_ranks: int32 [16, 16], replicated, may hold values from 16 to 96, as said below
- mute_start: int32 [8192, 64], P('tile'), may hold values from 0 to 127
- thresholds: float32 [64], replicated, may hold values from 0.05 to 0.5
Outputs:
- estimate: float32 [4, 8192, 128], P('freq', 'tile')
- misfit: float32 [4, 8192, 128], P('freq', 'tile')
The draws below stay inside these ranges and needn't reach their ends.
Inputs may be any that keep to these rules, and one draw needn't show every extreme that they name: `tile_ranks`: some tile has rank 96 and some rank 16.
All inputs are finite; a program needn't handle non-finite values.
Results may differ from the reference program's by a relative error of at most 0.013.
Values may be sent and summed in bfloat16 or wider, within the bound.
No kernel may reach another device: no remote copies, remote signals or barrier semaphores. Data moves between devices by JAX's collectives and lax.ppermute only.
A program may use at most 64 MiB of HBM per device.

```python
import math
import jax
import jax.numpy as jnp
from jax import lax

NB = 512
TSIDE = 16
N = 8192
RMAX = 96
RMIN = 16
S = 64
NF = 4
NT = 256
GROUP = 1
OUTER = 2
INNER = 1


def draw_tile_ranks(key, part):
    first_key, second_key = jax.random.split(jax.random.fold_in(key, 7))
    values = jax.random.randint(first_key, (TSIDE * TSIDE,), RMIN, RMAX + 1)
    spots = jax.random.permutation(second_key, TSIDE * TSIDE)
    values = values.at[spots[0]].set(RMAX).at[spots[1]].set(RMIN)
    return values.reshape(TSIDE, TSIDE).astype(jnp.int32)


def place_ends(entries, stream_key, low, largest):
    spot = [jax.random.randint(jax.random.fold_in(stream_key, axis), (), 0, length) for axis, length in enumerate(entries.shape)]
    widest = entries.shape.index(max(entries.shape))
    beside = spot[:widest] + [(spot[widest] + 1) % entries.shape[widest]] + spot[widest + 1:]
    return entries.at[tuple(spot)].set(low).at[tuple(beside)].set(largest)


def block_scale(own_key, extent, pieces, least, top_value):
    level, own = 1.0, jax.random.fold_in(own_key, 6)
    for position, blocks in pieces:
        heights = jnp.exp(jax.random.uniform(jax.random.fold_in(own, position), (blocks,), jnp.float32, least / len(pieces), top_value / len(pieces)))
        level = level * jnp.repeat(heights, extent[position] // blocks).reshape([-1 if axis == position else 1 for axis in range(len(extent))])
    return level


def normal_values(own_key, shape, deviation, limit, shards=(), held_as=jnp.bfloat16):
    drawn = jax.random.normal(own_key, shape, jnp.float32) * deviation
    if len(shards) > 0:
        drawn = block_scale(own_key, shape, shards, -0.22, 0.18) * drawn
    return jnp.clip(drawn, min=-limit, max=limit).astype(held_as)


def setup_inputs(seed: int = 0) -> dict:
    keys = jax.random.split(jax.random.key(seed), 8)
    return {
        "left_basis": normal_values(keys[0], (NF, N, 2, TSIDE * RMAX), (4 * TSIDE * RMAX) ** -0.5, 0.078125, ((0, 2), (1, 16))),
        "right_basis": normal_values(keys[1], (NF, N, 2, TSIDE * RMAX), NB ** -0.5, 0.25, ((0, 2), (1, 16))),
        "start_model": normal_values(keys[2], (NF, N, 2 * S), 0.5, 3.0, ((0, 2), (1, 16)), jnp.float32),
        "recorded": normal_values(keys[3], (NF, N, 2 * S), 1.0, 6.0, ((0, 2), (1, 16)), jnp.float32),
        "tile_ranks": draw_tile_ranks(jax.random.fold_in(keys[7], 71), 0),
        "mute_start": place_ends(jax.random.randint(keys[5], (N, S), 0, NT // 2), jax.random.fold_in(keys[5], 1), 0, (NT // 2) - 1).astype(jnp.int32),
        "thresholds": jnp.clip(jnp.exp(jax.random.uniform(keys[6], (S,), jnp.float32, math.log(0.05), math.log(0.5))), 0.05, 0.5),
    }


STEP_SIZE = 0.5

def phase_table():
    sample_index = jnp.arange(NT, dtype=jnp.int32)[:, None]
    bin_index = jnp.arange(NF, dtype=jnp.int32)[None, :] + NT // 4
    phases = (sample_index * bin_index % NT).astype(jnp.float32) * (2.0 * math.pi / NT)
    return jnp.stack([jnp.cos(phases), -jnp.sin(phases)])

def coefficients(basis, vector, rank_mask):
    sub_rows = N // TSIDE // GROUP
    blocks = basis.reshape(TSIDE, GROUP, sub_rows, 2, TSIDE * RMAX)
    vectors = vector.reshape(TSIDE, GROUP, sub_rows, 2 * S)

    def per_block(operands):
        tile_block, values, kept_mask = operands
        product = jnp.einsum('gnak,gnc->gakc', tile_block.astype(jnp.float32), values.astype(jnp.float32))
        real_part = product[:, 0, :, :S] + product[:, 1, :, S:]
        imag_part = product[:, 0, :, S:] - product[:, 1, :, :S]
        partial_value = jnp.concatenate([real_part, imag_part], 2).reshape(GROUP, TSIDE, RMAX, 2 * S)
        partial_value = partial_value * kept_mask[None, :, :, None]
        partial_value = lax.optimization_barrier(partial_value.astype(jnp.bfloat16)).astype(jnp.float32)
        return lax.optimization_barrier(jnp.sum(partial_value, 0)).astype(jnp.bfloat16)
    return lax.map(per_block, (blocks, vectors, rank_mask))

def expand(basis, coefficient):
    blocks = basis.reshape(TSIDE, N // TSIDE, 2, TSIDE * RMAX)

    def per_block(operands):
        tile_block, values = operands
        product = jnp.einsum('nak,kc->nac', tile_block.astype(jnp.float32), values.reshape(TSIDE * RMAX, 2 * S).astype(jnp.float32))
        real_part = product[:, 0, :S] - product[:, 1, S:]
        imag_part = product[:, 0, S:] + product[:, 1, :S]
        return jnp.concatenate([real_part, imag_part], 1)
    return lax.map(per_block, (blocks, coefficient)).reshape(N, 2 * S)

def sparsify(estimate, mute_start, thresholds):
    wave_table = phase_table()
    stacked = estimate.reshape(NF, N, 2, S)
    series = jnp.einsum('atk,knas->nst', wave_table, stacked, precision=lax.Precision.HIGHEST) / math.sqrt(NF)
    sample_index = jnp.arange(NT, dtype=jnp.int32)
    series = jnp.where(sample_index[None, None, :] >= mute_start[:, :, None], series, jnp.zeros_like(series))
    cutoff = thresholds[None, :, None]
    series = series - jnp.clip(series, -cutoff, cutoff)
    returned = jnp.einsum('nst,atk->knas', series, wave_table, precision=lax.Precision.HIGHEST) * (2.0 * math.sqrt(NF) / NT)
    return returned.reshape(NF, N, 2 * S)

def reference(left_basis, right_basis, start_model, recorded, tile_ranks, mute_start, thresholds):
    levels = jnp.arange(RMAX, dtype=jnp.int32)
    left_mask = (levels[None, None, :] < tile_ranks[:, :, None]).astype(jnp.float32)
    right_mask = jnp.transpose(left_mask, (1, 0, 2))

    def per_frequency(operands):
        left_one, right_one, estimate_one, recorded_one = operands
        forward = coefficients(right_one, estimate_one.astype(jnp.bfloat16), right_mask)
        misfit_one = expand(left_one, jnp.transpose(forward, (1, 0, 2, 3))) - recorded_one
        adjoint = coefficients(left_one, misfit_one.astype(jnp.bfloat16), left_mask)
        gradient = expand(right_one, jnp.transpose(adjoint, (1, 0, 2, 3)))
        return (estimate_one - STEP_SIZE * gradient, misfit_one)
    estimate = start_model
    misfit = recorded
    for outer_step in range(OUTER):
        for inner_step in range(INNER):
            estimate, misfit = lax.map(per_frequency, (left_basis, right_basis, estimate, recorded))
        estimate = sparsify(estimate, mute_start, thresholds)
    return (estimate, misfit)
```

```python
import math

import jax
import jax.numpy as jnp
from jax import lax
from jax.experimental import pallas as pl
from jax.experimental.pallas import tpu as pltpu
from jax.sharding import PartitionSpec as P

NT = 256
OUTER = 2
STEP_SIZE = 0.5


def lane_is_real(shape):
    return lax.broadcasted_iota(jnp.int32, shape, 1) < shape[1] // 2


def interleave(vector, scratch):
    rows, columns = vector.shape
    turned = pltpu.roll(vector, columns // 2, 1)
    turned = jnp.where(lane_is_real(vector.shape), turned, -turned)
    scratch[pl.ds(0, rows, stride=2), :] = vector
    scratch[pl.ds(1, rows, stride=2), :] = turned
    return scratch[...].astype(jnp.bfloat16)


def combine(scratch):
    rows = scratch.shape[0] // 2
    plain = scratch[pl.ds(0, rows, stride=2), :]
    turned = pltpu.roll(scratch[pl.ds(1, rows, stride=2), :], scratch.shape[1] // 2, 1)
    return plain + jnp.where(lane_is_real(plain.shape), -turned, turned)


def contract(basis, vectors, ranks, out):
    inside, slots, _ = out.shape
    product = lax.dot_general(
        basis, vectors, (((0,), (0,)), ((), ())), preferred_element_type=jnp.float32
    )
    level = lax.broadcasted_iota(jnp.int32, (slots, out.shape[2]), 0)
    for tile in range(inside):
        piece = product[tile * slots : (tile + 1) * slots]
        out[tile] = jnp.where(level < ranks[tile], piece, 0.0).astype(out.dtype)


def planes_as_rows(basis):
    height, planes, columns = basis.shape
    return basis.reshape(height * planes, columns)


def partials_kernel(ranks, basis, vector, out, pairs):
    vectors = interleave(vector[0].astype(jnp.float32), pairs)
    contract(planes_as_rows(basis[0]), vectors, ranks, out)


def partials(basis, vector, ranks, freq):
    _, height, planes, columns = basis.shape
    inside = ranks.shape[0]
    width = vector.shape[2]
    return pl.pallas_call(
        partials_kernel,
        grid=(1,),
        in_specs=[
            pl.BlockSpec(memory_space=pltpu.SMEM),
            pl.BlockSpec((1, height, planes, columns), lambda _: (freq, 0, 0, 0)),
            pl.BlockSpec((1, height, width), lambda _: (freq, 0, 0)),
        ],
        out_specs=pl.BlockSpec((inside, columns // inside, width), lambda _: (0, 0, 0)),
        out_shape=jax.ShapeDtypeStruct((inside, columns // inside, width), jnp.bfloat16),
        scratch_shapes=[pltpu.VMEM((height * planes, width), jnp.float32)],
        name="partials",
    )(ranks, basis, vector)


def residual_kernel(ranks, basis, coefficient, recorded, *rest):
    misfit, out, product, pairs = rest[-4:]
    rows = planes_as_rows(basis[0])
    inside, slots, width = coefficient.shape
    product[...] = jnp.dot(
        rows, coefficient[...].reshape(inside * slots, width), preferred_element_type=jnp.float32
    )
    value = combine(product) - recorded[0]
    misfit[0] = value
    contract(rows, interleave(value, pairs), ranks, out)


def residual(basis, coefficient, recorded, ranks, freq, before):
    freqs, height, planes, columns = basis.shape
    inside, slots, width = coefficient.shape
    operands = [ranks, basis, coefficient, recorded]
    in_specs = [
        pl.BlockSpec(memory_space=pltpu.SMEM),
        pl.BlockSpec((1, height, planes, columns), lambda _: (freq, 0, 0, 0)),
        pl.BlockSpec((inside, slots, width), lambda _: (0, 0, 0)),
        pl.BlockSpec((1, height, width), lambda _: (freq, 0, 0)),
    ]
    aliases = {}
    if before is not None:
        aliases = {len(operands): 0}
        operands.append(before)
        in_specs.append(pl.BlockSpec(memory_space=pl.ANY))
    return pl.pallas_call(
        residual_kernel,
        grid=(1,),
        in_specs=in_specs,
        out_specs=[
            pl.BlockSpec((1, height, width), lambda _: (freq, 0, 0)),
            pl.BlockSpec((inside, slots, width), lambda _: (0, 0, 0)),
        ],
        out_shape=[
            jax.ShapeDtypeStruct((freqs, height, width), jnp.float32),
            jax.ShapeDtypeStruct((inside, slots, width), jnp.bfloat16),
        ],
        scratch_shapes=[
            pltpu.VMEM((height * planes, width), jnp.float32),
            pltpu.VMEM((height * planes, width), jnp.float32),
        ],
        input_output_aliases=aliases,
        name="residual",
    )(*operands)


def update_kernel(basis, coefficient, model, out, product):
    inside, slots, width = coefficient.shape
    product[...] = jnp.dot(
        planes_as_rows(basis[0]),
        coefficient[...].reshape(inside * slots, width),
        preferred_element_type=jnp.float32,
    )
    out[...] = (model[0] - STEP_SIZE * combine(product)).astype(out.dtype)


def update(basis, coefficient, model, freq):
    _, height, planes, columns = basis.shape
    inside, slots, width = coefficient.shape
    return pl.pallas_call(
        update_kernel,
        grid=(1,),
        in_specs=[
            pl.BlockSpec((1, height, planes, columns), lambda _: (freq, 0, 0, 0)),
            pl.BlockSpec((inside, slots, width), lambda _: (0, 0, 0)),
            pl.BlockSpec((1, height, width), lambda _: (freq, 0, 0)),
        ],
        out_specs=pl.BlockSpec((height, width), lambda _: (0, 0)),
        out_shape=jax.ShapeDtypeStruct((height, width), jnp.bfloat16),
        scratch_shapes=[pltpu.VMEM((height * planes, width), jnp.float32)],
        name="update",
    )(basis, coefficient, model)


def sparsify_kernel(mute, cutoff, ahead, back, *rest):
    spread, (out, planes, returned) = rest[:-3], rest[-3:]
    freq_count = len(spread)
    rows, width = spread[0].shape
    half = rows // 2
    kept = out.shape[0]
    terms, sums = 2 * freq_count, returned.shape[0] // half
    is_real = lane_is_real((half, width))
    for k in range(freq_count):
        upper = spread[k][:half].astype(jnp.float32)
        lower = spread[k][half:].astype(jnp.float32)
        planes[pl.ds(2 * k, half, stride=terms), :] = jnp.where(
            is_real, upper, pltpu.roll(lower, width // 2, 1)
        )
        planes[pl.ds(2 * k + 1, half, stride=terms), :] = jnp.where(
            is_real, pltpu.roll(upper, width // 2, 1), lower
        )
    limit = jnp.concatenate([cutoff[...], cutoff[...]], 1)
    sample_index = lax.broadcasted_iota(jnp.int32, (NT // 2, 2 * width), 0)
    ahead_early, ahead_late = ahead[: NT // 2], ahead[NT // 2 :]

    def per_pair(step, _):
        first = 2 * step
        pair = planes[pl.ds(pl.multiple_of(first * terms, 2 * terms), 2 * terms), :]
        values = jnp.concatenate([pair[:terms], pair[terms:]], 1).astype(jnp.bfloat16)
        starts = jnp.concatenate([mute[pl.ds(first, 1), :], mute[pl.ds(first + 1, 1), :]], 1)
        early = jnp.dot(ahead_early, values, preferred_element_type=jnp.float32)
        late = jnp.dot(ahead_late, values, preferred_element_type=jnp.float32)
        early = early - jnp.clip(early, -limit, limit)
        early = jnp.where(sample_index >= starts, early, 0.0)
        late = late - jnp.clip(late, -limit, limit)
        series = jnp.concatenate([early, late], 0).astype(jnp.bfloat16)
        sums_here = jnp.dot(back[...], series, preferred_element_type=jnp.float32)
        returned[pl.ds(pl.multiple_of(first * sums, 2 * sums), 2 * sums), :] = jnp.concatenate(
            [sums_here[:, :width], sums_here[:, width:]], 0
        )
        return 0

    lax.fori_loop(0, half // 2, per_pair, 0, unroll=4)
    for k in range(kept):
        real_part = returned[pl.ds(2 * k, half, stride=sums), :]
        imag_part = returned[pl.ds(2 * k + 1, half, stride=sums), :]
        out[k, :half] = jnp.where(is_real, real_part, pltpu.roll(imag_part, width // 2, 1))
        out[k, half:] = jnp.where(is_real, pltpu.roll(real_part, width // 2, 1), imag_part)


def sparsify(spread, mute, cutoff, ahead, back, kept):
    rows, width = spread[0].shape
    terms, sums = 2 * len(spread), back.shape[0]
    return pl.pallas_call(
        sparsify_kernel,
        out_shape=jax.ShapeDtypeStruct((kept, rows, width), jnp.float32),
        scratch_shapes=[
            pltpu.VMEM((rows // 2 * terms, width), jnp.float32),
            pltpu.VMEM((rows // 2 * sums, width), jnp.float32),
        ],
        name="sparsify",
    )(mute, cutoff, ahead, back, *spread)


def wave_tables(freq_count, kept):
    sample_index = lax.iota(jnp.int32, NT)[:, None]
    order = (lax.iota(jnp.int32, freq_count) + kept * lax.axis_index("freq")) % freq_count
    phases = (sample_index * (order[None, :] + NT // 4) % NT).astype(jnp.float32)
    phases = phases * (2.0 * math.pi / NT)
    table = jnp.stack([jnp.cos(phases), -jnp.sin(phases)], 2).reshape(NT, 2 * freq_count)
    ahead = (table / math.sqrt(freq_count)).astype(jnp.bfloat16)
    sums = -(-2 * kept // 8) * 8
    back = (table[:, : 2 * kept] * (2.0 * math.sqrt(freq_count) / NT)).T
    back = jnp.pad(back, ((0, sums - 2 * kept), (0, 0))).astype(jnp.bfloat16)
    return ahead, back


def shuffle(partial_value):
    inside, slots, columns = partial_value.shape
    tile_count = lax.axis_size("tile")
    group_size = tile_count // inside
    if group_size == 1:
        return lax.all_to_all(partial_value, "tile", split_axis=0, concat_axis=0, tiled=True)
    outgoing = jnp.broadcast_to(partial_value[:, None], (inside, group_size, slots, columns))
    outgoing = outgoing.reshape(tile_count, slots, columns)
    incoming = lax.all_to_all(outgoing, "tile", split_axis=0, concat_axis=0, tiled=True)
    incoming = incoming.reshape(inside, group_size, slots, columns).astype(jnp.float32)
    return jnp.sum(incoming, 1).astype(jnp.bfloat16)


def from_others(value):
    size = lax.axis_size("freq")
    return [
        lax.ppermute(value, "freq", [((d + shift) % size, d) for d in range(size)])
        for shift in range(1, size)
    ]


def body(left_basis, right_basis, start_model, recorded, tile_ranks, mute_start, thresholds):
    tile_count = lax.axis_size("tile")
    inside = tile_ranks.shape[0]
    tile_block = lax.axis_index("tile") // (tile_count // inside)
    column_ranks = lax.dynamic_slice_in_dim(tile_ranks, tile_block, 1, 1).reshape(inside)
    row_ranks = lax.dynamic_slice_in_dim(tile_ranks, tile_block, 1, 0).reshape(inside)
    kept, height, width = start_model.shape
    freq_count = kept * lax.axis_size("freq")
    half = height // 2
    mute = jnp.concatenate([mute_start[:half], mute_start[half:]], 1)
    cutoff = jnp.tile(thresholds, 2)[None]
    ahead, back = wave_tables(freq_count, kept)
    freqs = range(kept)
    model = start_model
    for outer_step in range(OUTER):
        forward = [shuffle(partials(right_basis, model, column_ranks, f)) for f in freqs]
        misfit = None
        adjoint = []
        for f in freqs:
            misfit, outgoing = residual(left_basis, forward[f], recorded, row_ranks, f, misfit)
            adjoint.append(shuffle(outgoing))
        own, others = [], []
        for f in freqs:
            own.append(update(right_basis, adjoint[f], model, f))
            others.append(from_others(own[f]))
        spread = own + [others[f][d] for d in range(len(others[0])) for f in freqs]
        model = sparsify(spread, mute, cutoff, ahead, back, kept)
    return (model, misfit)


def solution(mesh):
    return jax.shard_map(
        body,
        mesh=mesh,
        in_specs=(
            P("freq", "tile", None, None),
            P("freq", "tile", None, None),
            P("freq", "tile", None),
            P("freq", "tile", None),
            P(),
            P("tile", None),
            P(),
        ),
        out_specs=(P("freq", "tile", None), P("freq", "tile", None)),
        check_vma=False,
    )
```

```python
import functools
import math

import jax
import jax.numpy as jnp
from jax import lax
from jax.experimental import pallas as pl
from jax.experimental.pallas import tpu as pltpu
from jax.sharding import PartitionSpec as P

NT = 256
OUTER = 2
STEP_SIZE = 0.5


def lane_is_real(shape):
    return lax.broadcasted_iota(jnp.int32, shape, 1) < shape[1] // 2


def interleave(vector, scratch):
    rows, columns = vector.shape
    turned = pltpu.roll(vector, columns // 2, 1)
    turned = jnp.where(lane_is_real(vector.shape), turned, -turned)
    scratch[pl.ds(0, rows, stride=2), :] = vector
    scratch[pl.ds(1, rows, stride=2), :] = turned
    return scratch[...].astype(jnp.bfloat16)


def combine(scratch):
    rows = scratch.shape[0] // 2
    plain = scratch[pl.ds(0, rows, stride=2), :]
    turned = pltpu.roll(scratch[pl.ds(1, rows, stride=2), :], scratch.shape[1] // 2, 1)
    return plain + jnp.where(lane_is_real(plain.shape), -turned, turned)


def planes_as_rows(basis):
    height, planes, columns = basis.shape
    return basis.reshape(height * planes, columns)


def whole():
    return pl.BlockSpec(memory_space=pltpu.VMEM)


def room(mebibytes):
    return pltpu.CompilerParams(vmem_limit_bytes=mebibytes * 2**20)


def block_of(inside):
    return lax.axis_index("tile") // (lax.axis_size("tile") // inside)


def expand(basis, coefficient, scratch):
    tiles, slots, width = coefficient.shape
    scratch[...] = jnp.dot(
        planes_as_rows(basis),
        coefficient.reshape(tiles * slots, width),
        preferred_element_type=jnp.float32,
    )
    return combine(scratch)


def contract(basis, vector, scratch, rank_of, out):
    tiles, slots, width = out.shape
    vectors = interleave(vector, scratch).T
    product = jnp.dot(vectors, planes_as_rows(basis), preferred_element_type=jnp.float32).T
    level = lax.broadcasted_iota(jnp.int32, (slots, width), 0)
    for tile in range(tiles):
        piece = product[tile * slots : (tile + 1) * slots]
        out[tile] = jnp.where(level < rank_of(tile), piece, 0.0).astype(out.dtype)


def partials_kernel(ranks, basis, vector, out, pairs):
    block = block_of(ranks.shape[0])
    for f in range(basis.shape[0]):
        contract(basis[f], vector[f], pairs, lambda tile: ranks[tile, block], out.at[:, f])


def partials(basis, vector, ranks):
    freqs, height, planes, columns = basis.shape
    inside, width = ranks.shape[0], vector.shape[2]
    return pl.pallas_call(
        partials_kernel,
        in_specs=[pl.BlockSpec(memory_space=pltpu.SMEM), whole(), whole()],
        out_specs=whole(),
        out_shape=jax.ShapeDtypeStruct((inside, freqs, columns // inside, width), jnp.bfloat16),
        scratch_shapes=[pltpu.VMEM((height * planes, width), jnp.float32)],
        compiler_params=room(12),
        name="partials",
    )(ranks, basis, vector)


def residual_kernel(ranks, basis, coefficient, recorded, misfit, out, product, pairs):
    block = block_of(ranks.shape[0])
    for f in range(basis.shape[0]):
        value = expand(basis[f], coefficient[:, f], product) - recorded[f]
        misfit[f] = value
        contract(basis[f], value, pairs, lambda tile: ranks[block, tile], out.at[:, f])


def residual(basis, coefficient, recorded, ranks):
    _, height, planes, _ = basis.shape
    scratch = pltpu.VMEM((height * planes, recorded.shape[2]), jnp.float32)
    return pl.pallas_call(
        residual_kernel,
        in_specs=[pl.BlockSpec(memory_space=pltpu.SMEM), whole(), whole(), whole()],
        out_specs=[whole(), whole()],
        out_shape=[
            jax.ShapeDtypeStruct(recorded.shape, jnp.float32),
            jax.ShapeDtypeStruct(coefficient.shape, jnp.bfloat16),
        ],
        scratch_shapes=[scratch, scratch],
        compiler_params=room(12),
        name="residual",
    )(ranks, basis, coefficient, recorded)


def update_kernel(freq, basis, coefficient, model, out, product):
    gradient = expand(basis[freq], coefficient[:, freq], product)
    out[...] = (model[freq] - STEP_SIZE * gradient).astype(out.dtype)


def update(basis, coefficient, model, freq):
    _, height, planes, _ = basis.shape
    width = model.shape[2]
    return pl.pallas_call(
        functools.partial(update_kernel, freq),
        in_specs=[whole(), whole(), whole()],
        out_specs=whole(),
        out_shape=jax.ShapeDtypeStruct((height, width), jnp.bfloat16),
        scratch_shapes=[pltpu.VMEM((height * planes, width), jnp.float32)],
        compiler_params=room(12),
        name="update",
    )(basis, coefficient, model)


def sparsify_kernel(mute, cutoff, ahead, back, *rest):
    spread, (out, planes, returned, wide, narrow) = rest[:-5], rest[-5:]
    freq_count = len(spread)
    rows, width = spread[0].shape
    half = rows // 2
    kept = out.shape[0]
    terms, sums = 2 * freq_count, returned.shape[0] // half
    is_real = lane_is_real((half, width))
    for k in range(freq_count):
        upper = spread[k][:half].astype(jnp.float32)
        lower = spread[k][half:].astype(jnp.float32)
        planes[pl.ds(2 * k, half, stride=terms), :] = jnp.where(
            is_real, upper, pltpu.roll(lower, width // 2, 1)
        )
        planes[pl.ds(2 * k + 1, half, stride=terms), :] = jnp.where(
            is_real, pltpu.roll(upper, width // 2, 1), lower
        )
    limit = cutoff[...]
    sample_index = lax.broadcasted_iota(jnp.int32, (NT // 2, width), 0)
    group = narrow.shape[1] // width

    def per_group(step, _):
        first = pl.multiple_of(step * group, group)
        block = planes[pl.ds(pl.multiple_of(first * terms, terms * group), terms * group), :]
        values = jnp.concatenate([block[r * terms : (r + 1) * terms] for r in range(group)], 1)
        wide[...] = jnp.dot(
            ahead[...], values.astype(jnp.bfloat16), preferred_element_type=jnp.float32
        )
        starts = mute[pl.ds(first, group), :]
        for r in range(group):
            lanes = pl.ds(r * width, width)
            early = wide[: NT // 2, lanes]
            late = wide[NT // 2 :, lanes]
            early = early - jnp.clip(early, -limit, limit)
            early = jnp.where(sample_index >= starts[r : r + 1], early, 0.0)
            late = late - jnp.clip(late, -limit, limit)
            narrow[: NT // 2, lanes] = early.astype(narrow.dtype)
            narrow[NT // 2 :, lanes] = late.astype(narrow.dtype)
        total = jnp.dot(back[...], narrow[...], preferred_element_type=jnp.float32)
        returned[pl.ds(pl.multiple_of(first * sums, sums * group), sums * group), :] = (
            jnp.concatenate([total[:, r * width : (r + 1) * width] for r in range(group)], 0)
        )
        return 0

    lax.fori_loop(0, half // group, per_group, 0)
    for k in range(kept):
        real_part = returned[pl.ds(2 * k, half, stride=sums), :]
        imag_part = returned[pl.ds(2 * k + 1, half, stride=sums), :]
        out[k, :half] = jnp.where(is_real, real_part, pltpu.roll(imag_part, width // 2, 1))
        out[k, half:] = jnp.where(is_real, pltpu.roll(real_part, width // 2, 1), imag_part)


def sparsify(spread, mute, cutoff, ahead, back, kept):
    rows, width = spread[0].shape
    terms, sums = 2 * len(spread), back.shape[0]
    group = math.gcd(rows // 2, 32)
    return pl.pallas_call(
        sparsify_kernel,
        out_shape=jax.ShapeDtypeStruct((kept, rows, width), jnp.float32),
        scratch_shapes=[
            pltpu.VMEM((rows // 2 * terms, width), jnp.float32),
            pltpu.VMEM((rows // 2 * sums, width), jnp.float32),
            pltpu.VMEM((NT, group * width), jnp.float32),
            pltpu.VMEM((NT, group * width), jnp.bfloat16),
        ],
        compiler_params=room(16),
        name="sparsify",
    )(mute, cutoff, ahead, back, *spread)


def wave(shape, sample_dim, freq_count, kept):
    entry = lax.broadcasted_iota(jnp.int32, shape, 1 - sample_dim)
    sample = lax.broadcasted_iota(jnp.int32, shape, sample_dim)
    order = lax.rem(lax.shift_right_logical(entry, 1) + kept * lax.axis_index("freq"), freq_count)
    turns = sample * (order + NT // 4) + (entry & 1) * (NT // 4)
    phases = lax.rem(turns, NT).astype(jnp.float32)
    return jnp.cos(phases * (2.0 * math.pi / NT))


def tables_kernel(kept, freq_count, mute_start, thresholds, mute, cutoff, ahead, back):
    starts = mute_start[...].T
    half = starts.shape[0] // 2
    mute[...] = jnp.concatenate([starts[:half], starts[half:]], 1)
    cutoff[...] = jnp.concatenate([thresholds[...], thresholds[...]], 1)
    ahead[...] = (wave(ahead.shape, 0, freq_count, kept) / math.sqrt(freq_count)).astype(
        ahead.dtype
    )
    scale = 2.0 * math.sqrt(freq_count) / NT
    back[...] = (wave(back.shape, 1, freq_count, kept) * scale).astype(back.dtype)


def tables(mute_start, thresholds, kept, freq_count):
    height, sources = mute_start.shape
    sums = -(-2 * kept // 8) * 8
    return pl.pallas_call(
        functools.partial(tables_kernel, kept, freq_count),
        in_specs=[whole(), whole()],
        out_specs=[whole()] * 4,
        out_shape=[
            jax.ShapeDtypeStruct((height // 2, 2 * sources), jnp.int32),
            jax.ShapeDtypeStruct((1, 2 * sources), jnp.float32),
            jax.ShapeDtypeStruct((NT, 2 * freq_count), jnp.bfloat16),
            jax.ShapeDtypeStruct((sums, NT), jnp.bfloat16),
        ],
        compiler_params=room(4),
        name="tables",
    )(mute_start.T, thresholds[None])


def shuffle(partial_value):
    inside, freqs, slots, columns = partial_value.shape
    tile_count = lax.axis_size("tile")
    group_size = tile_count // inside
    if group_size == 1:
        return lax.all_to_all(partial_value, "tile", split_axis=0, concat_axis=0, tiled=True)
    outgoing = jnp.broadcast_to(
        partial_value[:, None], (inside, group_size, freqs, slots, columns)
    )
    outgoing = outgoing.reshape(tile_count, freqs, slots, columns)
    incoming = lax.all_to_all(outgoing, "tile", split_axis=0, concat_axis=0, tiled=True)
    incoming = incoming.reshape(inside, group_size, freqs, slots, columns).astype(jnp.float32)
    return jnp.sum(incoming, 1).astype(jnp.bfloat16)


def from_others(value):
    size = lax.axis_size("freq")
    return [
        lax.ppermute(value, "freq", [((d + shift) % size, d) for d in range(size)])
        for shift in range(1, size)
    ]


def body(left_basis, right_basis, start_model, recorded, tile_ranks, mute_start, thresholds):
    kept = start_model.shape[0]
    freq_count = kept * lax.axis_size("freq")
    mute, cutoff, ahead, back = tables(mute_start, thresholds, kept, freq_count)
    freqs = range(kept)
    model = start_model
    for outer_step in range(OUTER):
        forward = shuffle(partials(right_basis, model, tile_ranks))
        misfit, outgoing = residual(left_basis, forward, recorded, tile_ranks)
        adjoint = shuffle(outgoing)
        own = [update(right_basis, adjoint, model, f) for f in freqs]
        others = [from_others(value) for value in own]
        spread = own + [others[f][d] for d in range(len(others[0])) for f in freqs]
        model = sparsify(spread, mute, cutoff, ahead, back, kept)
    return (model, misfit)


def solution(mesh):
    return jax.shard_map(
        body,
        mesh=mesh,
        in_specs=(
            P("freq", "tile", None, None),
            P("freq", "tile", None, None),
            P("freq", "tile", None),
            P("freq", "tile", None),
            P(),
            P("tile", None),
            P(),
        ),
        out_specs=(P("freq", "tile", None), P("freq", "tile", None)),
        check_vma=False,
    )
```

```python
import functools
import math

import jax
import jax.numpy as jnp
from jax import lax
from jax.experimental import pallas as pl
from jax.experimental.pallas import tpu as pltpu
from jax.sharding import PartitionSpec as P

NT = 256
OUTER = 2
STEP_SIZE = 0.5


def lane_is_real(shape):
    return lax.broadcasted_iota(jnp.int32, shape, 1) < shape[1] // 2


def interleave(vector, scratch):
    rows, columns = vector.shape
    turned = pltpu.roll(vector, columns // 2, 1)
    turned = jnp.where(lane_is_real(vector.shape), turned, -turned)
    scratch[pl.ds(0, rows, stride=2), :] = vector
    scratch[pl.ds(1, rows, stride=2), :] = turned
    return scratch[...].astype(jnp.bfloat16)


def combine(scratch):
    rows = scratch.shape[0] // 2
    plain = scratch[pl.ds(0, rows, stride=2), :]
    turned = pltpu.roll(scratch[pl.ds(1, rows, stride=2), :], scratch.shape[1] // 2, 1)
    return plain + jnp.where(lane_is_real(plain.shape), -turned, turned)


def planes_as_rows(basis):
    height, planes, columns = basis.shape
    return basis.reshape(height * planes, columns)


def whole():
    return pl.BlockSpec(memory_space=pltpu.VMEM)


def room(mebibytes):
    return pltpu.CompilerParams(vmem_limit_bytes=mebibytes * 2**20)


def block_of(inside):
    return lax.axis_index("tile") // (lax.axis_size("tile") // inside)


def expand(basis, coefficient, scratch):
    tiles, slots, width = coefficient.shape
    scratch[...] = jnp.dot(
        planes_as_rows(basis),
        coefficient.reshape(tiles * slots, width),
        preferred_element_type=jnp.float32,
    )
    return combine(scratch)


def contract(basis, vector, scratch, rank_of, out):
    tiles, slots, width = out.shape
    vectors = interleave(vector, scratch).T
    product = jnp.dot(vectors, planes_as_rows(basis), preferred_element_type=jnp.float32).T
    level = lax.broadcasted_iota(jnp.int32, (slots, width), 0)
    for tile in range(tiles):
        piece = product[tile * slots : (tile + 1) * slots]
        out[tile] = jnp.where(level < rank_of(tile), piece, 0.0).astype(out.dtype)


def partials_kernel(ranks, basis, vector, out, *pairs):
    block = block_of(ranks.shape[0])
    for f in range(basis.shape[0]):
        contract(basis[f], vector[f], pairs[f], lambda tile: ranks[tile, block], out.at[:, f])


def first_partials_kernel(
    ranks_from, basis_from, vector_from, out, ranks, basis, vector, rank_copied, copied, *pairs
):
    freqs = basis.shape[0]
    ranks_copy = pltpu.make_async_copy(ranks_from, ranks, rank_copied)
    copies = [
        [
            pltpu.make_async_copy(vector_from.at[f], vector.at[f], copied.at[0, f]),
            pltpu.make_async_copy(basis_from.at[f], basis.at[f], copied.at[1, f]),
        ]
        for f in range(freqs)
    ]
    for copy in [ranks_copy] + sum(copies, []):
        copy.start()
    ranks_copy.wait()
    block = block_of(ranks.shape[0])
    for f in range(freqs):
        for copy in copies[f]:
            copy.wait()
        contract(basis[f], vector[f], pairs[f], lambda tile: ranks[tile, block], out.at[:, f])


def partials(basis, vector, ranks, first):
    freqs, height, planes, columns = basis.shape
    inside, width = ranks.shape[0], vector.shape[2]
    scratch = [pltpu.VMEM((height * planes, width), jnp.float32)] * freqs
    if first:
        in_specs = [pl.BlockSpec(memory_space=pl.ANY)] * 3
        scratch = [
            pltpu.SMEM(ranks.shape, ranks.dtype),
            pltpu.VMEM(basis.shape, basis.dtype),
            pltpu.VMEM(vector.shape, vector.dtype),
            pltpu.SemaphoreType.DMA,
            pltpu.SemaphoreType.DMA((2, freqs)),
        ] + scratch
    else:
        in_specs = [pl.BlockSpec(memory_space=pltpu.SMEM), whole(), whole()]
    return pl.pallas_call(
        first_partials_kernel if first else partials_kernel,
        in_specs=in_specs,
        out_specs=whole(),
        out_shape=jax.ShapeDtypeStruct((inside, freqs, columns // inside, width), jnp.bfloat16),
        scratch_shapes=scratch,
        compiler_params=room(60 if first else 12),
        name="partials",
    )(ranks, basis, vector)


def residual_kernel(ranks, basis, coefficient, recorded, *rest):
    freqs = basis.shape[0]
    misfit, out, scratch = rest[: -1 - 2 * freqs], rest[-1 - 2 * freqs], rest[-2 * freqs :]
    block = block_of(ranks.shape[0])
    values = []
    for f in range(freqs):
        values.append(expand(basis[f], coefficient[:, f], scratch[f]) - recorded[f])
        if misfit:
            misfit[0][f] = values[f]
    for f in range(freqs):
        contract(
            basis[f], values[f], scratch[freqs + f], lambda tile: ranks[block, tile], out.at[:, f]
        )


def residual(basis, coefficient, recorded, ranks, last):
    freqs, height, planes, _ = basis.shape
    scratch = pltpu.VMEM((height * planes, recorded.shape[2]), jnp.float32)
    out_shape = [jax.ShapeDtypeStruct(coefficient.shape, jnp.bfloat16)]
    if last:
        out_shape.insert(0, jax.ShapeDtypeStruct(recorded.shape, jnp.float32))
    return pl.pallas_call(
        residual_kernel,
        in_specs=[pl.BlockSpec(memory_space=pltpu.SMEM), whole(), whole(), whole()],
        out_specs=[whole()] * len(out_shape),
        out_shape=out_shape,
        scratch_shapes=[scratch] * (2 * freqs),
        compiler_params=room(12),
        name="residual",
    )(ranks, basis, coefficient, recorded)


def update_kernel(freq, basis, coefficient, model, out, product):
    gradient = expand(basis[freq], coefficient[:, freq], product)
    out[...] = (model[freq] - STEP_SIZE * gradient).astype(out.dtype)


def update(basis, coefficient, model, freq):
    _, height, planes, _ = basis.shape
    width = model.shape[2]
    return pl.pallas_call(
        functools.partial(update_kernel, freq),
        in_specs=[whole(), whole(), whole()],
        out_specs=whole(),
        out_shape=jax.ShapeDtypeStruct((height, width), jnp.bfloat16),
        scratch_shapes=[pltpu.VMEM((height * planes, width), jnp.float32)],
        compiler_params=room(12),
        name="update",
    )(basis, coefficient, model)


def sparsify_kernel(mute, cutoff, ahead, back, *rest):
    spread, (out, planes, returned, wide, narrow) = rest[:-5], rest[-5:]
    freq_count = len(spread)
    rows, width = spread[0].shape
    half = rows // 2
    kept = out.shape[0]
    terms, sums = 2 * freq_count, returned.shape[0] // half
    is_real = lane_is_real((half, width))
    for k in range(freq_count):
        upper = spread[k][:half].astype(jnp.float32)
        lower = spread[k][half:].astype(jnp.float32)
        planes[pl.ds(2 * k, half, stride=terms), :] = jnp.where(
            is_real, upper, pltpu.roll(lower, width // 2, 1)
        )
        planes[pl.ds(2 * k + 1, half, stride=terms), :] = jnp.where(
            is_real, pltpu.roll(upper, width // 2, 1), lower
        )
    limit = cutoff[...]
    sample_index = lax.broadcasted_iota(jnp.int32, (NT // 2, width), 0)
    group = narrow.shape[1] // width

    def per_group(step, _):
        first = pl.multiple_of(step * group, group)
        block = planes[pl.ds(pl.multiple_of(first * terms, terms * group), terms * group), :]
        values = jnp.concatenate([block[r * terms : (r + 1) * terms] for r in range(group)], 1)
        wide[...] = jnp.dot(
            ahead[...], values.astype(jnp.bfloat16), preferred_element_type=jnp.float32
        )
        starts = mute[pl.ds(first, group), :]
        for r in range(group):
            lanes = pl.ds(r * width, width)
            early = wide[: NT // 2, lanes]
            late = wide[NT // 2 :, lanes]
            early = early - jnp.clip(early, -limit, limit)
            early = jnp.where(sample_index >= starts[r : r + 1], early, 0.0)
            late = late - jnp.clip(late, -limit, limit)
            narrow[: NT // 2, lanes] = early.astype(narrow.dtype)
            narrow[NT // 2 :, lanes] = late.astype(narrow.dtype)
        total = jnp.dot(back[...], narrow[...], preferred_element_type=jnp.float32)
        returned[pl.ds(pl.multiple_of(first * sums, sums * group), sums * group), :] = (
            jnp.concatenate([total[:, r * width : (r + 1) * width] for r in range(group)], 0)
        )
        return 0

    lax.fori_loop(0, half // group, per_group, 0)
    for k in range(kept):
        real_part = returned[pl.ds(2 * k, half, stride=sums), :]
        imag_part = returned[pl.ds(2 * k + 1, half, stride=sums), :]
        out[k, :half] = jnp.where(is_real, real_part, pltpu.roll(imag_part, width // 2, 1))
        out[k, half:] = jnp.where(is_real, pltpu.roll(real_part, width // 2, 1), imag_part)


def sparsify(spread, mute, cutoff, ahead, back, kept):
    rows, width = spread[0].shape
    terms, sums = 2 * len(spread), back.shape[0]
    group = math.gcd(rows // 2, 32)
    return pl.pallas_call(
        sparsify_kernel,
        out_shape=jax.ShapeDtypeStruct((kept, rows, width), jnp.float32),
        scratch_shapes=[
            pltpu.VMEM((rows // 2 * terms, width), jnp.float32),
            pltpu.VMEM((rows // 2 * sums, width), jnp.float32),
            pltpu.VMEM((NT, group * width), jnp.float32),
            pltpu.VMEM((NT, group * width), jnp.bfloat16),
        ],
        compiler_params=room(16),
        name="sparsify",
    )(mute, cutoff, ahead, back, *spread)


def wave(shape, sample_dim, freq_count, kept):
    entry = lax.broadcasted_iota(jnp.int32, shape, 1 - sample_dim)
    sample = lax.broadcasted_iota(jnp.int32, shape, sample_dim)
    order = lax.rem(lax.shift_right_logical(entry, 1) + kept * lax.axis_index("freq"), freq_count)
    turns = sample * (order + NT // 4) + (entry & 1) * (NT // 4)
    phases = lax.rem(turns, NT).astype(jnp.float32)
    return jnp.cos(phases * (2.0 * math.pi / NT))


def tables_kernel(kept, freq_count, mute_start, thresholds, mute, cutoff, ahead, back):
    starts = mute_start[...].T
    half = starts.shape[0] // 2
    mute[...] = jnp.concatenate([starts[:half], starts[half:]], 1)
    cutoff[...] = jnp.concatenate([thresholds[...], thresholds[...]], 1)
    ahead[...] = (wave(ahead.shape, 0, freq_count, kept) / math.sqrt(freq_count)).astype(
        ahead.dtype
    )
    scale = 2.0 * math.sqrt(freq_count) / NT
    back[...] = (wave(back.shape, 1, freq_count, kept) * scale).astype(back.dtype)


def tables(mute_start, thresholds, kept, freq_count):
    height, sources = mute_start.shape
    sums = -(-2 * kept // 8) * 8
    return pl.pallas_call(
        functools.partial(tables_kernel, kept, freq_count),
        in_specs=[whole(), whole()],
        out_specs=[whole()] * 4,
        out_shape=[
            jax.ShapeDtypeStruct((height // 2, 2 * sources), jnp.int32),
            jax.ShapeDtypeStruct((1, 2 * sources), jnp.float32),
            jax.ShapeDtypeStruct((NT, 2 * freq_count), jnp.bfloat16),
            jax.ShapeDtypeStruct((sums, NT), jnp.bfloat16),
        ],
        compiler_params=room(4),
        name="tables",
    )(mute_start.T, thresholds[None])


def shuffle(partial_value):
    inside, freqs, slots, columns = partial_value.shape
    tile_count = lax.axis_size("tile")
    group_size = tile_count // inside
    if group_size == 1:
        return lax.all_to_all(partial_value, "tile", split_axis=0, concat_axis=0, tiled=True)
    outgoing = jnp.broadcast_to(
        partial_value[:, None], (inside, group_size, freqs, slots, columns)
    )
    outgoing = outgoing.reshape(tile_count, freqs, slots, columns)
    incoming = lax.all_to_all(outgoing, "tile", split_axis=0, concat_axis=0, tiled=True)
    incoming = incoming.reshape(inside, group_size, freqs, slots, columns).astype(jnp.float32)
    return jnp.sum(incoming, 1).astype(jnp.bfloat16)


def from_others(value):
    size = lax.axis_size("freq")
    return [
        lax.ppermute(value, "freq", [((d + shift) % size, d) for d in range(size)])
        for shift in range(1, size)
    ]


def body(left_basis, right_basis, start_model, recorded, tile_ranks, mute_start, thresholds):
    kept = start_model.shape[0]
    freq_count = kept * lax.axis_size("freq")
    mute, cutoff, ahead, back = tables(mute_start, thresholds, kept, freq_count)
    freqs = range(kept)
    model = start_model
    for outer_step in range(OUTER):
        forward = shuffle(partials(right_basis, model, tile_ranks, outer_step == 0))
        *misfit, outgoing = residual(
            left_basis, forward, recorded, tile_ranks, outer_step == OUTER - 1
        )
        adjoint = shuffle(outgoing)
        own = [update(right_basis, adjoint, model, f) for f in freqs]
        others = [from_others(value) for value in own]
        spread = own + [others[f][d] for d in range(len(others[0])) for f in freqs]
        model = sparsify(spread, mute, cutoff, ahead, back, kept)
    return (model, misfit[0])


def solution(mesh):
    return jax.shard_map(
        body,
        mesh=mesh,
        in_specs=(
            P("freq", "tile", None, None),
            P("freq", "tile", None, None),
            P("freq", "tile", None),
            P("freq", "tile", None),
            P(),
            P("tile", None),
            P(),
        ),
        out_specs=(P("freq", "tile", None), P("freq", "tile", None)),
        check_vma=False,
    )
```

```python
import functools
import math

import jax
import jax.numpy as jnp
from jax import lax
from jax.experimental import pallas as pl
from jax.experimental.pallas import tpu as pltpu
from jax.sharding import PartitionSpec as P

NT = 256
OUTER = 2
STEP_SIZE = 0.5
PIECES = 2


def lane_is_real(shape):
    return lax.broadcasted_iota(jnp.int32, shape, 1) < shape[1] // 2


def interleave(vector, scratch):
    rows, columns = vector.shape
    turned = pltpu.roll(vector, columns // 2, 1)
    turned = jnp.where(lane_is_real(vector.shape), turned, -turned)
    scratch[pl.ds(0, rows, stride=2), :] = vector
    scratch[pl.ds(1, rows, stride=2), :] = turned
    return scratch[...].astype(jnp.bfloat16)


def combine(scratch):
    rows = scratch.shape[0] // 2
    plain = scratch[pl.ds(0, rows, stride=2), :]
    turned = pltpu.roll(scratch[pl.ds(1, rows, stride=2), :], scratch.shape[1] // 2, 1)
    return plain + jnp.where(lane_is_real(plain.shape), -turned, turned)


def planes_as_rows(basis):
    height, planes, columns = basis.shape
    return basis.reshape(height * planes, columns)


def whole():
    return pl.BlockSpec(memory_space=pltpu.VMEM)


def room(mebibytes):
    return pltpu.CompilerParams(vmem_limit_bytes=mebibytes * 2**20)


def block_of(inside):
    return lax.axis_index("tile") // (lax.axis_size("tile") // inside)


def expand(basis, coefficient, scratch):
    tiles, slots, width = coefficient.shape
    scratch[...] = jnp.dot(
        planes_as_rows(basis),
        coefficient.reshape(tiles * slots, width),
        preferred_element_type=jnp.float32,
    )
    return combine(scratch)


def contract(basis, vector, scratch, rank_of, out):
    tiles, slots, width = out.shape
    vectors = interleave(vector, scratch).T
    product = jnp.dot(vectors, planes_as_rows(basis), preferred_element_type=jnp.float32).T
    level = lax.broadcasted_iota(jnp.int32, (slots, width), 0)
    for tile in range(tiles):
        piece = product[tile * slots : (tile + 1) * slots]
        out[tile] = jnp.where(level < rank_of(tile), piece, 0.0).astype(out.dtype)


def partials_kernel(ranks, basis, *rest):
    freqs = basis.shape[0]
    pieces, out, pairs = rest[: -1 - freqs], rest[-1 - freqs], rest[-freqs:]
    block = block_of(ranks.shape[0])
    for f in range(freqs):
        vector = jnp.concatenate([piece[f] for piece in pieces], 0)
        contract(basis[f], vector, pairs[f], lambda tile: ranks[tile, block], out.at[:, f])


def first_partials_kernel(
    ranks_from, basis_from, vector_from, out, ranks, basis, vector, rank_copied, copied, *pairs
):
    freqs = basis.shape[0]
    ranks_copy = pltpu.make_async_copy(ranks_from, ranks, rank_copied)
    copies = [
        [
            pltpu.make_async_copy(vector_from.at[f], vector.at[f], copied.at[0, f]),
            pltpu.make_async_copy(basis_from.at[f], basis.at[f], copied.at[1, f]),
        ]
        for f in range(freqs)
    ]
    for copy in [ranks_copy] + sum(copies, []):
        copy.start()
    ranks_copy.wait()
    block = block_of(ranks.shape[0])
    for f in range(freqs):
        for copy in copies[f]:
            copy.wait()
        contract(basis[f], vector[f], pairs[f], lambda tile: ranks[tile, block], out.at[:, f])


def partials(basis, pieces, ranks, first):
    freqs, height, planes, columns = basis.shape
    inside, width = ranks.shape[0], pieces[0].shape[2]
    scratch = [pltpu.VMEM((height * planes, width), jnp.float32)] * freqs
    if first:
        in_specs = [pl.BlockSpec(memory_space=pl.ANY)] * 3
        scratch = [
            pltpu.SMEM(ranks.shape, ranks.dtype),
            pltpu.VMEM(basis.shape, basis.dtype),
            pltpu.VMEM(pieces[0].shape, pieces[0].dtype),
            pltpu.SemaphoreType.DMA,
            pltpu.SemaphoreType.DMA((2, freqs)),
        ] + scratch
    else:
        in_specs = [pl.BlockSpec(memory_space=pltpu.SMEM), whole()] + [whole()] * len(pieces)
    return pl.pallas_call(
        first_partials_kernel if first else partials_kernel,
        in_specs=in_specs,
        out_specs=whole(),
        out_shape=jax.ShapeDtypeStruct((inside, freqs, columns // inside, width), jnp.bfloat16),
        scratch_shapes=scratch,
        compiler_params=room(60 if first else 12),
        name="partials",
    )(ranks, basis, *pieces)


def residual_kernel(ranks, basis, coefficient, recorded, *rest):
    freqs = basis.shape[0]
    misfit, out, scratch = rest[: -1 - 2 * freqs], rest[-1 - 2 * freqs], rest[-2 * freqs :]
    block = block_of(ranks.shape[0])
    values = []
    for f in range(freqs):
        values.append(expand(basis[f], coefficient[:, f], scratch[f]) - recorded[f])
        if misfit:
            misfit[0][f] = values[f]
    for f in range(freqs):
        contract(
            basis[f], values[f], scratch[freqs + f], lambda tile: ranks[block, tile], out.at[:, f]
        )


def residual(basis, coefficient, recorded, ranks, last):
    freqs, height, planes, _ = basis.shape
    scratch = pltpu.VMEM((height * planes, recorded.shape[2]), jnp.float32)
    out_shape = [jax.ShapeDtypeStruct(coefficient.shape, jnp.bfloat16)]
    if last:
        out_shape.insert(0, jax.ShapeDtypeStruct(recorded.shape, jnp.float32))
    return pl.pallas_call(
        residual_kernel,
        in_specs=[pl.BlockSpec(memory_space=pltpu.SMEM), whole(), whole(), whole()],
        out_specs=[whole()] * len(out_shape),
        out_shape=out_shape,
        scratch_shapes=[scratch] * (2 * freqs),
        compiler_params=room(12),
        name="residual",
    )(ranks, basis, coefficient, recorded)


def update_kernel(first_row, model_row, basis, coefficient, model, out, *scratch):
    freqs, rows, _ = out.shape
    for f in range(freqs):
        part = basis[f, first_row : first_row + rows]
        gradient = expand(part, coefficient[:, f], scratch[f])
        before = model[f, model_row : model_row + rows]
        out[f] = (before - STEP_SIZE * gradient).astype(out.dtype)


def update(basis, coefficient, model, first_row, rows, model_row):
    freqs, _, planes, _ = basis.shape
    width = model.shape[2]
    return pl.pallas_call(
        functools.partial(update_kernel, first_row, model_row),
        in_specs=[whole(), whole(), whole()],
        out_specs=whole(),
        out_shape=jax.ShapeDtypeStruct((freqs, rows, width), jnp.bfloat16),
        scratch_shapes=[pltpu.VMEM((rows * planes, width), jnp.float32)] * freqs,
        compiler_params=room(12),
        name="update",
    )(basis, coefficient, model)


def sparsify_body(first_pair, mute, cutoff, ahead, back, arrays, out, planes, returned, wide, narrow):
    kept, rows, width = arrays[0].shape
    spread = [array.at[f] for array in arrays for f in range(kept)]
    freq_count = len(spread)
    half = rows // 2
    terms, sums = 2 * freq_count, returned.shape[0] // half
    is_real = lane_is_real((half, width))
    for k in range(freq_count):
        upper = spread[k][:half].astype(jnp.float32)
        lower = spread[k][half:].astype(jnp.float32)
        planes[pl.ds(2 * k, half, stride=terms), :] = jnp.where(
            is_real, upper, pltpu.roll(lower, width // 2, 1)
        )
        planes[pl.ds(2 * k + 1, half, stride=terms), :] = jnp.where(
            is_real, pltpu.roll(upper, width // 2, 1), lower
        )
    limit = cutoff[...]
    sample_index = lax.broadcasted_iota(jnp.int32, (NT // 2, width), 0)
    group = narrow.shape[1] // width

    def per_group(step, _):
        first = pl.multiple_of(step * group, group)
        block = planes[pl.ds(pl.multiple_of(first * terms, terms * group), terms * group), :]
        values = jnp.concatenate([block[r * terms : (r + 1) * terms] for r in range(group)], 1)
        wide[...] = jnp.dot(
            ahead[...], values.astype(jnp.bfloat16), preferred_element_type=jnp.float32
        )
        starts = mute[pl.ds(pl.multiple_of(first_pair + first, group), group), :]
        for r in range(group):
            lanes = pl.ds(r * width, width)
            early = wide[: NT // 2, lanes]
            late = wide[NT // 2 :, lanes]
            early = early - jnp.clip(early, -limit, limit)
            early = jnp.where(sample_index >= starts[r : r + 1], early, 0.0)
            late = late - jnp.clip(late, -limit, limit)
            narrow[: NT // 2, lanes] = early.astype(narrow.dtype)
            narrow[NT // 2 :, lanes] = late.astype(narrow.dtype)
        total = jnp.dot(back[...], narrow[...], preferred_element_type=jnp.float32)
        returned[pl.ds(pl.multiple_of(first * sums, sums * group), sums * group), :] = (
            jnp.concatenate([total[:, r * width : (r + 1) * width] for r in range(group)], 0)
        )
        return 0

    lax.fori_loop(0, half // group, per_group, 0)
    for k in range(kept):
        real_part = returned[pl.ds(2 * k, half, stride=sums), :]
        imag_part = returned[pl.ds(2 * k + 1, half, stride=sums), :]
        out[k, :half] = jnp.where(is_real, real_part, pltpu.roll(imag_part, width // 2, 1))
        out[k, half:] = jnp.where(is_real, pltpu.roll(real_part, width // 2, 1), imag_part)


def sparsify_kernel(first_pair, mute, cutoff, ahead, back, *rest):
    sparsify_body(first_pair, mute, cutoff, ahead, back, rest[:-5], *rest[-5:])


def sparsify_into_kernel(first_pair, has_before, mute, cutoff, ahead, back, *rest):
    arrays, out, (piece, stored), scratch = rest[:-7], rest[-7], rest[-6:-4], rest[-4:]
    if has_before:
        arrays = arrays[:-1]
    sparsify_body(first_pair, mute, cutoff, ahead, back, arrays, piece, *scratch)
    rows = piece.shape[1]
    copy = pltpu.make_async_copy(piece, out.at[:, pl.ds(2 * first_pair, rows)], stored)
    copy.start()
    copy.wait()


def sparsify(arrays, mute, cutoff, ahead, back, piece, height=None, before=None):
    kept, rows, width = arrays[0].shape
    terms, sums = 2 * kept * len(arrays), back.shape[0]
    group = math.gcd(rows // 2, 32)
    scratch = [
        pltpu.VMEM((rows // 2 * terms, width), jnp.float32),
        pltpu.VMEM((rows // 2 * sums, width), jnp.float32),
        pltpu.VMEM((NT, group * width), jnp.float32),
        pltpu.VMEM((NT, group * width), jnp.bfloat16),
    ]
    operands = [mute, cutoff, ahead, back, *arrays]
    in_specs = [whole()] * len(operands)
    first_pair = piece * rows // 2
    aliases = {}
    if height is None:
        kernel = functools.partial(sparsify_kernel, first_pair)
        out_spec, out_rows = whole(), rows
    else:
        kernel = functools.partial(sparsify_into_kernel, first_pair, before is not None)
        out_spec, out_rows = pl.BlockSpec(memory_space=pl.ANY), height
        scratch = [pltpu.VMEM((kept, rows, width), jnp.float32), pltpu.SemaphoreType.DMA] + scratch
        if before is not None:
            aliases = {len(operands): 0}
            operands.append(before)
            in_specs.append(pl.BlockSpec(memory_space=pl.ANY))
    return pl.pallas_call(
        kernel,
        in_specs=in_specs,
        out_specs=out_spec,
        out_shape=jax.ShapeDtypeStruct((kept, out_rows, width), jnp.float32),
        scratch_shapes=scratch,
        input_output_aliases=aliases,
        compiler_params=room(16),
        name="sparsify",
    )(*operands)


def wave(shape, sample_dim, freq_count, kept):
    entry = lax.broadcasted_iota(jnp.int32, shape, 1 - sample_dim)
    sample = lax.broadcasted_iota(jnp.int32, shape, sample_dim)
    order = lax.rem(lax.shift_right_logical(entry, 1) + kept * lax.axis_index("freq"), freq_count)
    turns = sample * (order + NT // 4) + (entry & 1) * (NT // 4)
    phases = lax.rem(turns, NT).astype(jnp.float32)
    return jnp.cos(phases * (2.0 * math.pi / NT))


def tables_kernel(kept, freq_count, mute_start, thresholds, mute, cutoff, ahead, back):
    starts = mute_start[...].T
    half = starts.shape[0] // PIECES // 2
    for piece in range(PIECES):
        both = starts[2 * half * piece : 2 * half * (piece + 1)]
        mute[half * piece : half * (piece + 1)] = jnp.concatenate([both[:half], both[half:]], 1)
    cutoff[...] = jnp.concatenate([thresholds[...], thresholds[...]], 1)
    ahead[...] = (wave(ahead.shape, 0, freq_count, kept) / math.sqrt(freq_count)).astype(
        ahead.dtype
    )
    scale = 2.0 * math.sqrt(freq_count) / NT
    back[...] = (wave(back.shape, 1, freq_count, kept) * scale).astype(back.dtype)


def tables(mute_start, thresholds, kept, freq_count):
    height, sources = mute_start.shape
    sums = -(-2 * kept // 8) * 8
    return pl.pallas_call(
        functools.partial(tables_kernel, kept, freq_count),
        in_specs=[whole(), whole()],
        out_specs=[whole()] * 4,
        out_shape=[
            jax.ShapeDtypeStruct((height // 2, 2 * sources), jnp.int32),
            jax.ShapeDtypeStruct((1, 2 * sources), jnp.float32),
            jax.ShapeDtypeStruct((NT, 2 * freq_count), jnp.bfloat16),
            jax.ShapeDtypeStruct((sums, NT), jnp.bfloat16),
        ],
        compiler_params=room(4),
        name="tables",
    )(mute_start.T, thresholds[None])


def shuffle(partial_value):
    inside, freqs, slots, columns = partial_value.shape
    tile_count = lax.axis_size("tile")
    group_size = tile_count // inside
    if group_size == 1:
        return lax.all_to_all(partial_value, "tile", split_axis=0, concat_axis=0, tiled=True)
    outgoing = jnp.broadcast_to(
        partial_value[:, None], (inside, group_size, freqs, slots, columns)
    )
    outgoing = outgoing.reshape(tile_count, freqs, slots, columns)
    incoming = lax.all_to_all(outgoing, "tile", split_axis=0, concat_axis=0, tiled=True)
    incoming = incoming.reshape(inside, group_size, freqs, slots, columns).astype(jnp.float32)
    return jnp.sum(incoming, 1).astype(jnp.bfloat16)


def from_others(value):
    size = lax.axis_size("freq")
    return [
        lax.ppermute(value, "freq", [((d + shift) % size, d) for d in range(size)])
        for shift in range(1, size)
    ]


def body(left_basis, right_basis, start_model, recorded, tile_ranks, mute_start, thresholds):
    kept = start_model.shape[0]
    freq_count = kept * lax.axis_size("freq")
    mute, cutoff, ahead, back = tables(mute_start, thresholds, kept, freq_count)
    height = start_model.shape[1]
    rows = height // PIECES
    model = [start_model]
    for outer_step in range(OUTER):
        first, last = outer_step == 0, outer_step == OUTER - 1
        forward = shuffle(partials(right_basis, model, tile_ranks, first))
        *misfit, outgoing = residual(left_basis, forward, recorded, tile_ranks, last)
        adjoint = shuffle(outgoing)
        spread = []
        for piece in range(PIECES):
            row = piece * rows
            before, before_row = (model[0], row) if first else (model[piece], 0)
            own = update(right_basis, adjoint, before, row, rows, before_row)
            spread.append([own] + from_others(own))
        if last:
            estimate = None
            for piece in range(PIECES):
                estimate = sparsify(
                    spread[piece], mute, cutoff, ahead, back, piece, height, estimate
                )
        else:
            model = [
                sparsify(spread[piece], mute, cutoff, ahead, back, piece)
                for piece in range(PIECES)
            ]
    return (estimate, misfit[0])


def solution(mesh):
    return jax.shard_map(
        body,
        mesh=mesh,
        in_specs=(
            P("freq", "tile", None, None),
            P("freq", "tile", None, None),
            P("freq", "tile", None),
            P("freq", "tile", None),
            P(),
            P("tile", None),
            P(),
        ),
        out_specs=(P("freq", "tile", None), P("freq", "tile", None)),
        check_vma=False,
    )
```

```python
import functools
import math

import jax
import jax.numpy as jnp
from jax import lax
from jax.experimental import pallas as pl
from jax.experimental.pallas import tpu as pltpu
from jax.sharding import PartitionSpec as P


NT = 256
OUTER = 2
STEP_SIZE = 0.5


def pieces_of(height):
    quarter = height // 4
    return [(0, quarter), (quarter, quarter), (2 * quarter, height - 2 * quarter)]


def lane_is_real(shape):
    return lax.broadcasted_iota(jnp.int32, shape, 1) < shape[1] // 2


def interleave(vector, scratch):
    rows, columns = vector.shape
    turned = pltpu.roll(vector, columns // 2, 1)
    turned = jnp.where(lane_is_real(vector.shape), turned, -turned)
    scratch[pl.ds(0, rows, stride=2), :] = vector
    scratch[pl.ds(1, rows, stride=2), :] = turned
    return scratch[...].astype(jnp.bfloat16)


def combine(scratch):
    rows = scratch.shape[0] // 2
    plain = scratch[pl.ds(0, rows, stride=2), :]
    turned = pltpu.roll(scratch[pl.ds(1, rows, stride=2), :], scratch.shape[1] // 2, 1)
    return plain + jnp.where(lane_is_real(plain.shape), -turned, turned)


def planes_as_rows(basis):
    height, planes, columns = basis.shape
    return basis.reshape(height * planes, columns)


def whole():
    return pl.BlockSpec(memory_space=pltpu.VMEM)


def room(mebibytes):
    return pltpu.CompilerParams(vmem_limit_bytes=mebibytes * 2**20)


def block_of(inside):
    return lax.axis_index("tile") // (lax.axis_size("tile") // inside)


def expand(basis, coefficient, scratch):
    tiles, slots, width = coefficient.shape
    scratch[...] = jnp.dot(
        planes_as_rows(basis),
        coefficient.reshape(tiles * slots, width),
        preferred_element_type=jnp.float32,
    )
    return combine(scratch)


def contract(basis, vector, scratch, rank_of, out):
    tiles, slots, width = out.shape
    vectors = interleave(vector, scratch).T
    product = jnp.dot(vectors, planes_as_rows(basis), preferred_element_type=jnp.float32).T
    level = lax.broadcasted_iota(jnp.int32, (slots, width), 0)
    for tile in range(tiles):
        piece = product[tile * slots : (tile + 1) * slots]
        out[tile] = jnp.where(level < rank_of(tile), piece, 0.0).astype(out.dtype)


def partials_kernel(ranks, basis, *rest):
    freqs = basis.shape[0]
    pieces, out, pairs = rest[: -1 - freqs], rest[-1 - freqs], rest[-freqs:]
    block = block_of(ranks.shape[0])
    for f in range(freqs):
        vector = jnp.concatenate([piece[f] for piece in pieces], 0)
        contract(basis[f], vector, pairs[f], lambda tile: ranks[tile, block], out.at[:, f])


def first_partials_kernel(
    ranks_from, basis_from, vector_from, out, ranks, basis, vector, rank_copied, copied, *pairs
):
    freqs = basis.shape[0]
    ranks_copy = pltpu.make_async_copy(ranks_from, ranks, rank_copied)
    copies = [
        [
            pltpu.make_async_copy(vector_from.at[f], vector.at[f], copied.at[0, f]),
            pltpu.make_async_copy(basis_from.at[f], basis.at[f], copied.at[1, f]),
        ]
        for f in range(freqs)
    ]
    for copy in [ranks_copy] + sum(copies, []):
        copy.start()
    ranks_copy.wait()
    block = block_of(ranks.shape[0])
    for f in range(freqs):
        for copy in copies[f]:
            copy.wait()
        contract(basis[f], vector[f], pairs[f], lambda tile: ranks[tile, block], out.at[:, f])


def partials(basis, pieces, ranks, first):
    freqs, height, planes, columns = basis.shape
    inside, width = ranks.shape[0], pieces[0].shape[2]
    scratch = [pltpu.VMEM((height * planes, width), jnp.float32)] * freqs
    if first:
        in_specs = [pl.BlockSpec(memory_space=pl.ANY)] * 3
        scratch = [
            pltpu.SMEM(ranks.shape, ranks.dtype),
            pltpu.VMEM(basis.shape, basis.dtype),
            pltpu.VMEM(pieces[0].shape, pieces[0].dtype),
            pltpu.SemaphoreType.DMA,
            pltpu.SemaphoreType.DMA((2, freqs)),
        ] + scratch
    else:
        in_specs = [pl.BlockSpec(memory_space=pltpu.SMEM), whole()] + [whole()] * len(pieces)
    return pl.pallas_call(
        first_partials_kernel if first else partials_kernel,
        in_specs=in_specs,
        out_specs=whole(),
        out_shape=jax.ShapeDtypeStruct((inside, freqs, columns // inside, width), jnp.bfloat16),
        scratch_shapes=scratch,
        compiler_params=room(60 if first else 12),
        name="partials",
    )(ranks, basis, *pieces)


def residual_kernel(ranks, basis, coefficient, recorded, out, *scratch):
    freqs = basis.shape[0]
    block = block_of(ranks.shape[0])
    values = [
        expand(basis[f], coefficient[:, f], scratch[f]) - recorded[f] for f in range(freqs)
    ]
    for f in range(freqs):
        contract(
            basis[f], values[f], scratch[freqs + f], lambda tile: ranks[block, tile], out.at[:, f]
        )


def last_residual_kernel(ranks, basis, coefficient, recorded, misfit, out, held, stored, *scratch):
    freqs = basis.shape[0]
    block = block_of(ranks.shape[0])
    copies = [
        pltpu.make_async_copy(held.at[f], misfit.at[f], stored.at[f]) for f in range(freqs)
    ]
    for f in range(freqs):
        held[f] = expand(basis[f], coefficient[:, f], scratch[f]) - recorded[f]
        copies[f].start()
    for f in range(freqs):
        contract(
            basis[f], held[f], scratch[freqs + f], lambda tile: ranks[block, tile], out.at[:, f]
        )
    for copy in copies:
        copy.wait()


def residual(basis, coefficient, recorded, ranks, last):
    freqs, height, planes, _ = basis.shape
    scratch = [pltpu.VMEM((height * planes, recorded.shape[2]), jnp.float32)] * (2 * freqs)
    out_specs = [whole()]
    out_shape = [jax.ShapeDtypeStruct(coefficient.shape, jnp.bfloat16)]
    if last:
        out_specs.insert(0, pl.BlockSpec(memory_space=pl.ANY))
        out_shape.insert(0, jax.ShapeDtypeStruct(recorded.shape, jnp.float32))
        scratch = [
            pltpu.VMEM(recorded.shape, jnp.float32),
            pltpu.SemaphoreType.DMA((freqs,)),
        ] + scratch
    return pl.pallas_call(
        last_residual_kernel if last else residual_kernel,
        in_specs=[pl.BlockSpec(memory_space=pltpu.SMEM), whole(), whole(), whole()],
        out_specs=out_specs,
        out_shape=out_shape,
        scratch_shapes=scratch,
        compiler_params=room(12),
        name="residual",
    )(ranks, basis, coefficient, recorded)


def update_kernel(first_row, model_row, basis, coefficient, model, *rest):
    freqs = basis.shape[0]
    out, scratch = rest[-1 - freqs], rest[-freqs:]
    rows = out.shape[1]
    for f in range(freqs):
        part = basis[f, first_row : first_row + rows]
        gradient = expand(part, coefficient[:, f], scratch[f])
        before = model[f, model_row : model_row + rows]
        out[f] = (before - STEP_SIZE * gradient).astype(out.dtype)


def update(basis, coefficient, model, first_row, rows, model_row):
    freqs, _, planes, _ = basis.shape
    width = model.shape[2]
    return pl.pallas_call(
        functools.partial(update_kernel, first_row, model_row),
        in_specs=[whole(), whole(), whole()],
        out_specs=whole(),
        out_shape=jax.ShapeDtypeStruct((freqs, rows, width), jnp.bfloat16),
        scratch_shapes=[pltpu.VMEM((rows * planes, width), jnp.float32)] * freqs,
        compiler_params=room(12),
        name="update",
    )(basis, coefficient, model)


def sparsify_body(
    first_pair,
    mute,
    cutoff,
    ahead,
    back,
    arrays,
    out,
    planes,
    returned,
    wide,
    narrow,
    finished=lambda f: None,
):
    kept, rows, width = arrays[0].shape
    spread = [array.at[f] for array in arrays for f in range(kept)]
    freq_count = len(spread)
    half = rows // 2
    terms, sums = 2 * freq_count, returned.shape[0] // half
    is_real = lane_is_real((half, width))
    for k in range(freq_count):
        upper = spread[k][:half].astype(jnp.float32)
        lower = spread[k][half:].astype(jnp.float32)
        planes[pl.ds(2 * k, half, stride=terms), :] = jnp.where(
            is_real, upper, pltpu.roll(lower, width // 2, 1)
        )
        planes[pl.ds(2 * k + 1, half, stride=terms), :] = jnp.where(
            is_real, pltpu.roll(upper, width // 2, 1), lower
        )
    limit = cutoff[...]
    sample_index = lax.broadcasted_iota(jnp.int32, (NT // 2, width), 0)
    group = narrow.shape[1] // width

    def per_group(step, _):
        first = pl.multiple_of(step * group, group)
        block = planes[pl.ds(pl.multiple_of(first * terms, terms * group), terms * group), :]
        values = jnp.concatenate([block[r * terms : (r + 1) * terms] for r in range(group)], 1)
        wide[...] = jnp.dot(
            ahead[...], values.astype(jnp.bfloat16), preferred_element_type=jnp.float32
        )
        starts = mute[pl.ds(pl.multiple_of(first_pair + first, group), group), :]
        for r in range(group):
            lanes = pl.ds(r * width, width)
            early = wide[: NT // 2, lanes]
            late = wide[NT // 2 :, lanes]
            early = early - jnp.clip(early, -limit, limit)
            early = jnp.where(sample_index >= starts[r : r + 1], early, 0.0)
            late = late - jnp.clip(late, -limit, limit)
            narrow[: NT // 2, lanes] = early.astype(narrow.dtype)
            narrow[NT // 2 :, lanes] = late.astype(narrow.dtype)
        total = jnp.dot(back[...], narrow[...], preferred_element_type=jnp.float32)
        returned[pl.ds(pl.multiple_of(first * sums, sums * group), sums * group), :] = (
            jnp.concatenate([total[:, r * width : (r + 1) * width] for r in range(group)], 0)
        )
        return 0

    lax.fori_loop(0, half // group, per_group, 0)
    for k in range(kept):
        real_part = returned[pl.ds(2 * k, half, stride=sums), :]
        imag_part = returned[pl.ds(2 * k + 1, half, stride=sums), :]
        out[k, :half] = jnp.where(is_real, real_part, pltpu.roll(imag_part, width // 2, 1))
        out[k, half:] = jnp.where(is_real, pltpu.roll(real_part, width // 2, 1), imag_part)
        finished(k)


def sparsify_kernel(first_pair, mute, cutoff, ahead, back, *rest):
    sparsify_body(first_pair, mute, cutoff, ahead, back, rest[:-5], *rest[-5:])


def sparsify_last_kernel(earlier_rows, first_pair, mute, cutoff, ahead, back, *rest):
    count = len(earlier_rows)
    arrays, earlier = rest[: -7 - count], rest[-7 - count : -7]
    out, piece, stored, *scratch = rest[-7:]
    kept, rows, _ = piece.shape
    copies = []
    for place, (row, value) in enumerate(zip(earlier_rows, earlier)):
        target = out.at[:, pl.ds(row, value.shape[1])]
        copies.append(pltpu.make_async_copy(value, target, stored.at[kept + place]))
        copies[-1].start()
    own = [
        pltpu.make_async_copy(piece.at[f], out.at[f, pl.ds(2 * first_pair, rows)], stored.at[f])
        for f in range(kept)
    ]
    sparsify_body(
        first_pair, mute, cutoff, ahead, back, arrays, piece, *scratch, lambda f: own[f].start()
    )
    for copy in copies + own:
        copy.wait()


def sparsify(arrays, mute, cutoff, ahead, back, row, height=None, earlier=()):
    kept, rows, width = arrays[0].shape
    terms, sums = 2 * kept * len(arrays), back.shape[0]
    group = math.gcd(rows // 2, 32)
    scratch = [
        pltpu.VMEM((rows // 2 * terms, width), jnp.float32),
        pltpu.VMEM((rows // 2 * sums, width), jnp.float32),
        pltpu.VMEM((NT, group * width), jnp.float32),
        pltpu.VMEM((NT, group * width), jnp.bfloat16),
    ]
    operands = [mute, cutoff, ahead, back, *arrays]
    if height is None:
        kernel = functools.partial(sparsify_kernel, row // 2)
        out_spec, out_rows = whole(), rows
    else:
        kernel = functools.partial(sparsify_last_kernel, [first for first, _ in earlier], row // 2)
        operands += [value for _, value in earlier]
        out_spec, out_rows = pl.BlockSpec(memory_space=pl.ANY), height
        scratch = [
            pltpu.VMEM((kept, rows, width), jnp.float32),
            pltpu.SemaphoreType.DMA((kept + len(earlier),)),
        ] + scratch
    return pl.pallas_call(
        kernel,
        in_specs=[whole()] * len(operands),
        out_specs=out_spec,
        out_shape=jax.ShapeDtypeStruct((kept, out_rows, width), jnp.float32),
        scratch_shapes=scratch,
        compiler_params=room(16),
        name="sparsify",
    )(*operands)


def wave(shape, sample_dim, freq_count, kept):
    entry = lax.broadcasted_iota(jnp.int32, shape, 1 - sample_dim)
    sample = lax.broadcasted_iota(jnp.int32, shape, sample_dim)
    order = lax.rem(lax.shift_right_logical(entry, 1) + kept * lax.axis_index("freq"), freq_count)
    turns = sample * (order + NT // 4) + (entry & 1) * (NT // 4)
    phases = lax.rem(turns, NT).astype(jnp.float32)
    return jnp.cos(phases * (2.0 * math.pi / NT))


def tables_kernel(kept, freq_count, mute_start, thresholds, mute, cutoff, ahead, back):
    starts = mute_start[...].T
    for row, rows in pieces_of(starts.shape[0]):
        upper, lower = starts[row : row + rows // 2], starts[row + rows // 2 : row + rows]
        mute[row // 2 : (row + rows) // 2] = jnp.concatenate([upper, lower], 1)
    cutoff[...] = jnp.concatenate([thresholds[...], thresholds[...]], 1)
    ahead[...] = (wave(ahead.shape, 0, freq_count, kept) / math.sqrt(freq_count)).astype(
        ahead.dtype
    )
    scale = 2.0 * math.sqrt(freq_count) / NT
    back[...] = (wave(back.shape, 1, freq_count, kept) * scale).astype(back.dtype)


def tables(mute_start, thresholds, kept, freq_count):
    height, sources = mute_start.shape
    sums = -(-2 * kept // 8) * 8
    return pl.pallas_call(
        functools.partial(tables_kernel, kept, freq_count),
        in_specs=[whole(), whole()],
        out_specs=[whole()] * 4,
        out_shape=[
            jax.ShapeDtypeStruct((height // 2, 2 * sources), jnp.int32),
            jax.ShapeDtypeStruct((1, 2 * sources), jnp.float32),
            jax.ShapeDtypeStruct((NT, 2 * freq_count), jnp.bfloat16),
            jax.ShapeDtypeStruct((sums, NT), jnp.bfloat16),
        ],
        compiler_params=room(4),
        name="tables",
    )(mute_start.T, thresholds[None])


def shuffle(partial_value):
    inside, freqs, slots, columns = partial_value.shape
    tile_count = lax.axis_size("tile")
    group_size = tile_count // inside
    if group_size == 1:
        return lax.all_to_all(partial_value, "tile", split_axis=0, concat_axis=0, tiled=True)
    outgoing = jnp.broadcast_to(
        partial_value[:, None], (inside, group_size, freqs, slots, columns)
    )
    outgoing = outgoing.reshape(tile_count, freqs, slots, columns)
    incoming = lax.all_to_all(outgoing, "tile", split_axis=0, concat_axis=0, tiled=True)
    incoming = incoming.reshape(inside, group_size, freqs, slots, columns).astype(jnp.float32)
    return jnp.sum(incoming, 1).astype(jnp.bfloat16)


def from_others(value):
    size = lax.axis_size("freq")
    return [
        lax.ppermute(value, "freq", [((d + shift) % size, d) for d in range(size)])
        for shift in range(1, size)
    ]


def body(left_basis, right_basis, start_model, recorded, tile_ranks, mute_start, thresholds):
    kept = start_model.shape[0]
    freq_count = kept * lax.axis_size("freq")
    mute, cutoff, ahead, back = tables(mute_start, thresholds, kept, freq_count)
    height = start_model.shape[1]
    pieces = pieces_of(height)
    model = [start_model]
    for outer_step in range(OUTER):
        first, last = outer_step == 0, outer_step == OUTER - 1
        forward = shuffle(partials(right_basis, model, tile_ranks, first))
        *misfit, outgoing = residual(left_basis, forward, recorded, tile_ranks, last)
        adjoint = shuffle(outgoing)
        spread = []
        for piece, (row, rows) in enumerate(pieces):
            before, before_row = (model[0], row) if first else (model[piece], 0)
            own = update(right_basis, adjoint, before, row, rows, before_row)
            spread.append([own] + from_others(own))
        model = []
        for arrays, (row, rows) in zip(spread, pieces):
            whole_height, earlier = None, []
            if last and row + rows == height:
                whole_height = height
                earlier = [(first_row, value) for (first_row, _), value in zip(pieces, model)]
            model.append(
                sparsify(arrays, mute, cutoff, ahead, back, row, whole_height, earlier)
            )
    return (model[-1], misfit[0])


def solution(mesh):
    return jax.shard_map(
        body,
        mesh=mesh,
        in_specs=(
            P("freq", "tile", None, None),
            P("freq", "tile", None, None),
            P("freq", "tile", None),
            P("freq", "tile", None),
            P(),
            P("tile", None),
            P(),
        ),
        out_specs=(P("freq", "tile", None), P("freq", "tile", None)),
        check_vma=False,
    )
```

```python
import functools
import math

import jax
import jax.numpy as jnp
from jax import lax
from jax.experimental import pallas as pl
from jax.experimental.pallas import tpu as pltpu
from jax.sharding import PartitionSpec as P


NT = 256
OUTER = 2
STEP_SIZE = 0.5


def pieces_of(height):
    quarter = height // 4
    return [(0, quarter), (quarter, quarter), (2 * quarter, height - 2 * quarter)]


def lane_is_real(shape):
    return lax.broadcasted_iota(jnp.int32, shape, 1) < shape[1] // 2


def interleave(vector, scratch):
    rows, columns = vector.shape
    turned = pltpu.roll(vector, columns // 2, 1)
    turned = jnp.where(lane_is_real(vector.shape), turned, -turned)
    scratch[pl.ds(0, rows, stride=2), :] = vector
    scratch[pl.ds(1, rows, stride=2), :] = turned
    return scratch[...].astype(jnp.bfloat16)


def combine(scratch):
    rows = scratch.shape[0] // 2
    plain = scratch[pl.ds(0, rows, stride=2), :]
    turned = pltpu.roll(scratch[pl.ds(1, rows, stride=2), :], scratch.shape[1] // 2, 1)
    return plain + jnp.where(lane_is_real(plain.shape), -turned, turned)


def planes_as_rows(basis):
    height, planes, columns = basis.shape
    return basis.reshape(height * planes, columns)


def whole():
    return pl.BlockSpec(memory_space=pltpu.VMEM)


def room(mebibytes):
    return pltpu.CompilerParams(vmem_limit_bytes=mebibytes * 2**20)


def block_of(inside):
    return lax.axis_index("tile") // (lax.axis_size("tile") // inside)


def expand(basis, coefficient, scratch):
    tiles, slots, width = coefficient.shape
    scratch[...] = jnp.dot(
        planes_as_rows(basis),
        coefficient.reshape(tiles * slots, width),
        preferred_element_type=jnp.float32,
    )
    return combine(scratch)


def contract(basis, vector, scratch, rank_of, out):
    tiles, slots, width = out.shape
    vectors = interleave(vector, scratch).T
    product = jnp.dot(vectors, planes_as_rows(basis), preferred_element_type=jnp.float32).T
    level = lax.broadcasted_iota(jnp.int32, (slots, width), 0)
    for tile in range(tiles):
        piece = product[tile * slots : (tile + 1) * slots]
        out[tile] = jnp.where(level < rank_of(tile), piece, 0.0).astype(out.dtype)


def partials_kernel(ranks, basis, *rest):
    freqs = basis.shape[0]
    pieces, out, pairs = rest[: -1 - freqs], rest[-1 - freqs], rest[-freqs:]
    block = block_of(ranks.shape[0])
    for f in range(freqs):
        vector = jnp.concatenate([piece[f] for piece in pieces], 0)
        contract(basis[f], vector, pairs[f], lambda tile: ranks[tile, block], out.at[:, f])


def first_partials_kernel(
    ranks_from, basis_from, vector_from, out, ranks, basis, vector, rank_copied, copied, *pairs
):
    freqs = basis.shape[0]
    ranks_copy = pltpu.make_async_copy(ranks_from, ranks, rank_copied)
    copies = [
        [
            pltpu.make_async_copy(vector_from.at[f], vector.at[f], copied.at[0, f]),
            pltpu.make_async_copy(basis_from.at[f], basis.at[f], copied.at[1, f]),
        ]
        for f in range(freqs)
    ]
    for copy in [ranks_copy] + sum(copies, []):
        copy.start()
    ranks_copy.wait()
    block = block_of(ranks.shape[0])
    for f in range(freqs):
        for copy in copies[f]:
            copy.wait()
        contract(basis[f], vector[f], pairs[f], lambda tile: ranks[tile, block], out.at[:, f])


def partials(basis, pieces, ranks, first):
    freqs, height, planes, columns = basis.shape
    inside, width = ranks.shape[0], pieces[0].shape[2]
    scratch = [pltpu.VMEM((height * planes, width), jnp.float32)] * freqs
    if first:
        in_specs = [pl.BlockSpec(memory_space=pl.ANY)] * 3
        scratch = [
            pltpu.SMEM(ranks.shape, ranks.dtype),
            pltpu.VMEM(basis.shape, basis.dtype),
            pltpu.VMEM(pieces[0].shape, pieces[0].dtype),
            pltpu.SemaphoreType.DMA,
            pltpu.SemaphoreType.DMA((2, freqs)),
        ] + scratch
    else:
        in_specs = [pl.BlockSpec(memory_space=pltpu.SMEM), whole()] + [whole()] * len(pieces)
    return pl.pallas_call(
        first_partials_kernel if first else partials_kernel,
        in_specs=in_specs,
        out_specs=whole(),
        out_shape=jax.ShapeDtypeStruct((inside, freqs, columns // inside, width), jnp.bfloat16),
        scratch_shapes=scratch,
        compiler_params=room(54 if first else 12),
        name="partials",
    )(ranks, basis, *pieces)


def residual_kernel(ranks, basis, coefficient, recorded, out, *scratch):
    freqs = basis.shape[0]
    block = block_of(ranks.shape[0])
    values = [
        expand(basis[f], coefficient[:, f], scratch[f]) - recorded[f] for f in range(freqs)
    ]
    for f in range(freqs):
        contract(
            basis[f], values[f], scratch[freqs + f], lambda tile: ranks[block, tile], out.at[:, f]
        )


def last_residual_kernel(ranks, basis, coefficient, recorded, misfit, out, held, stored, *scratch):
    freqs = basis.shape[0]
    block = block_of(ranks.shape[0])
    copies = [
        pltpu.make_async_copy(held.at[f], misfit.at[f], stored.at[f]) for f in range(freqs)
    ]
    for f in range(freqs):
        held[f] = expand(basis[f], coefficient[:, f], scratch[f]) - recorded[f]
        copies[f].start()
    for f in range(freqs):
        contract(
            basis[f], held[f], scratch[freqs + f], lambda tile: ranks[block, tile], out.at[:, f]
        )
    for copy in copies:
        copy.wait()


def residual(basis, coefficient, recorded, ranks, last):
    freqs, height, planes, _ = basis.shape
    scratch = [pltpu.VMEM((height * planes, recorded.shape[2]), jnp.float32)] * (2 * freqs)
    out_specs = [whole()]
    out_shape = [jax.ShapeDtypeStruct(coefficient.shape, jnp.bfloat16)]
    if last:
        out_specs.insert(0, pl.BlockSpec(memory_space=pl.ANY))
        out_shape.insert(0, jax.ShapeDtypeStruct(recorded.shape, jnp.float32))
        scratch = [
            pltpu.VMEM(recorded.shape, jnp.float32),
            pltpu.SemaphoreType.DMA((freqs,)),
        ] + scratch
    return pl.pallas_call(
        last_residual_kernel if last else residual_kernel,
        in_specs=[pl.BlockSpec(memory_space=pltpu.SMEM), whole(), whole(), whole()],
        out_specs=out_specs,
        out_shape=out_shape,
        scratch_shapes=scratch,
        compiler_params=room(12),
        name="residual",
    )(ranks, basis, coefficient, recorded)


def update_kernel(first_row, model_row, basis, coefficient, model, *rest):
    freqs = basis.shape[0]
    out, scratch = rest[-1 - freqs], rest[-freqs:]
    rows = out.shape[1]
    for f in range(freqs):
        part = basis[f, first_row : first_row + rows]
        gradient = expand(part, coefficient[:, f], scratch[f])
        before = model[f, model_row : model_row + rows]
        out[f] = (before - STEP_SIZE * gradient).astype(out.dtype)


def update(basis, coefficient, model, first_row, rows, model_row):
    freqs, _, planes, _ = basis.shape
    width = model.shape[2]
    return pl.pallas_call(
        functools.partial(update_kernel, first_row, model_row),
        in_specs=[whole(), whole(), whole()],
        out_specs=whole(),
        out_shape=jax.ShapeDtypeStruct((freqs, rows, width), jnp.bfloat16),
        scratch_shapes=[pltpu.VMEM((rows * planes, width), jnp.float32)] * freqs,
        compiler_params=room(12),
        name="update",
    )(basis, coefficient, model)


def sparsify_body(
    first_pair,
    mute,
    cutoff,
    ahead,
    back,
    arrays,
    out,
    planes,
    returned,
    wide,
    narrow,
    finished=lambda f: None,
):
    kept, rows, width = arrays[0].shape
    spread = [array.at[f] for array in arrays for f in range(kept)]
    freq_count = len(spread)
    half = rows // 2
    terms, sums = 2 * freq_count, returned.shape[0] // half
    is_real = lane_is_real((half, width))
    for k in range(freq_count):
        upper = spread[k][:half].astype(jnp.float32)
        lower = spread[k][half:].astype(jnp.float32)
        planes[pl.ds(2 * k, half, stride=terms), :] = jnp.where(
            is_real, upper, pltpu.roll(lower, width // 2, 1)
        )
        planes[pl.ds(2 * k + 1, half, stride=terms), :] = jnp.where(
            is_real, pltpu.roll(upper, width // 2, 1), lower
        )
    limit = cutoff[...]
    sample_index = lax.broadcasted_iota(jnp.int32, (NT // 2, width), 0)
    group = narrow.shape[1] // width

    def per_group(step, _):
        first = pl.multiple_of(step * group, group)
        block = planes[pl.ds(pl.multiple_of(first * terms, terms * group), terms * group), :]
        values = jnp.concatenate([block[r * terms : (r + 1) * terms] for r in range(group)], 1)
        wide[...] = jnp.dot(
            ahead[...], values.astype(jnp.bfloat16), preferred_element_type=jnp.float32
        )
        starts = mute[pl.ds(pl.multiple_of(first_pair + first, group), group), :]
        for r in range(group):
            lanes = pl.ds(r * width, width)
            early = wide[: NT // 2, lanes]
            late = wide[NT // 2 :, lanes]
            early = early - jnp.clip(early, -limit, limit)
            early = jnp.where(sample_index >= starts[r : r + 1], early, 0.0)
            late = late - jnp.clip(late, -limit, limit)
            narrow[: NT // 2, lanes] = early.astype(narrow.dtype)
            narrow[NT // 2 :, lanes] = late.astype(narrow.dtype)
        total = jnp.dot(back[...], narrow[...], preferred_element_type=jnp.float32)
        returned[pl.ds(pl.multiple_of(first * sums, sums * group), sums * group), :] = (
            jnp.concatenate([total[:, r * width : (r + 1) * width] for r in range(group)], 0)
        )
        return 0

    lax.fori_loop(0, half // group, per_group, 0)
    for k in range(kept):
        real_part = returned[pl.ds(2 * k, half, stride=sums), :]
        imag_part = returned[pl.ds(2 * k + 1, half, stride=sums), :]
        out[k, :half] = jnp.where(is_real, real_part, pltpu.roll(imag_part, width // 2, 1))
        out[k, half:] = jnp.where(is_real, pltpu.roll(real_part, width // 2, 1), imag_part)
        finished(k)


def sparsify_kernel(first_pair, mute, cutoff, ahead, back, *rest):
    sparsify_body(first_pair, mute, cutoff, ahead, back, rest[:-5], *rest[-5:])


def sparsify_last_kernel(earlier_rows, first_pair, mute, cutoff, ahead, back, *rest):
    count = len(earlier_rows)
    arrays, earlier = rest[: -7 - count], rest[-7 - count : -7]
    out, piece, stored, *scratch = rest[-7:]
    kept, rows, _ = piece.shape
    copies = []
    for place, (row, value) in enumerate(zip(earlier_rows, earlier)):
        target = out.at[:, pl.ds(row, value.shape[1])]
        copies.append(pltpu.make_async_copy(value, target, stored.at[kept + place]))
        copies[-1].start()
    own = [
        pltpu.make_async_copy(piece.at[f], out.at[f, pl.ds(2 * first_pair, rows)], stored.at[f])
        for f in range(kept)
    ]
    sparsify_body(
        first_pair, mute, cutoff, ahead, back, arrays, piece, *scratch, lambda f: own[f].start()
    )
    for copy in copies + own:
        copy.wait()


def sparsify(arrays, mute, cutoff, ahead, back, row, height=None, earlier=()):
    kept, rows, width = arrays[0].shape
    terms, sums = 2 * kept * len(arrays), back.shape[0]
    group = math.gcd(rows // 2, 32)
    scratch = [
        pltpu.VMEM((rows // 2 * terms, width), jnp.float32),
        pltpu.VMEM((rows // 2 * sums, width), jnp.float32),
        pltpu.VMEM((NT, group * width), jnp.float32),
        pltpu.VMEM((NT, group * width), jnp.bfloat16),
    ]
    operands = [mute, cutoff, ahead, back, *arrays]
    if height is None:
        kernel = functools.partial(sparsify_kernel, row // 2)
        out_spec, out_rows = whole(), rows
    else:
        kernel = functools.partial(sparsify_last_kernel, [first for first, _ in earlier], row // 2)
        operands += [value for _, value in earlier]
        out_spec, out_rows = pl.BlockSpec(memory_space=pl.ANY), height
        scratch = [
            pltpu.VMEM((kept, rows, width), jnp.float32),
            pltpu.SemaphoreType.DMA((kept + len(earlier),)),
        ] + scratch
    return pl.pallas_call(
        kernel,
        in_specs=[whole()] * len(operands),
        out_specs=out_spec,
        out_shape=jax.ShapeDtypeStruct((kept, out_rows, width), jnp.float32),
        scratch_shapes=scratch,
        compiler_params=room(16),
        name="sparsify",
    )(*operands)


def wave(shape, sample_dim, freq_count, kept):
    entry = lax.broadcasted_iota(jnp.int32, shape, 1 - sample_dim)
    sample = lax.broadcasted_iota(jnp.int32, shape, sample_dim)
    order = lax.rem(lax.shift_right_logical(entry, 1) + kept * lax.axis_index("freq"), freq_count)
    turns = sample * (order + NT // 4) + (entry & 1) * (NT // 4)
    phases = lax.rem(turns, NT).astype(jnp.float32)
    return jnp.cos(phases * (2.0 * math.pi / NT))


def tables_kernel(kept, freq_count, mute_start, thresholds, _, mute, cutoff, ahead, back):
    starts = mute_start[...].T
    for row, rows in pieces_of(starts.shape[0]):
        upper, lower = starts[row : row + rows // 2], starts[row + rows // 2 : row + rows]
        mute[row // 2 : (row + rows) // 2] = jnp.concatenate([upper, lower], 1)
    cutoff[...] = jnp.concatenate([thresholds[...], thresholds[...]], 1)
    ahead[...] = (wave(ahead.shape, 0, freq_count, kept) / math.sqrt(freq_count)).astype(
        ahead.dtype
    )
    scale = 2.0 * math.sqrt(freq_count) / NT
    back[...] = (wave(back.shape, 1, freq_count, kept) * scale).astype(back.dtype)


def tables(mute_start, thresholds, after, kept, freq_count):
    height, sources = mute_start.shape
    sums = -(-2 * kept // 8) * 8
    return pl.pallas_call(
        functools.partial(tables_kernel, kept, freq_count),
        in_specs=[whole(), whole(), pl.BlockSpec(memory_space=pl.ANY)],
        out_specs=[whole()] * 4,
        out_shape=[
            jax.ShapeDtypeStruct((height // 2, 2 * sources), jnp.int32),
            jax.ShapeDtypeStruct((1, 2 * sources), jnp.float32),
            jax.ShapeDtypeStruct((NT, 2 * freq_count), jnp.bfloat16),
            jax.ShapeDtypeStruct((sums, NT), jnp.bfloat16),
        ],
        compiler_params=room(4),
        cost_estimate=pl.CostEstimate(flops=4 * 10**9, transcendentals=0, bytes_accessed=2**23),
        name="tables",
    )(mute_start.T, thresholds[None], after)


def shuffle(partial_value):
    inside, freqs, slots, columns = partial_value.shape
    tile_count = lax.axis_size("tile")
    group_size = tile_count // inside
    if group_size == 1:
        return lax.all_to_all(partial_value, "tile", split_axis=0, concat_axis=0, tiled=True)
    outgoing = jnp.broadcast_to(
        partial_value[:, None], (inside, group_size, freqs, slots, columns)
    )
    outgoing = outgoing.reshape(tile_count, freqs, slots, columns)
    incoming = lax.all_to_all(outgoing, "tile", split_axis=0, concat_axis=0, tiled=True)
    incoming = incoming.reshape(inside, group_size, freqs, slots, columns).astype(jnp.float32)
    return jnp.sum(incoming, 1).astype(jnp.bfloat16)


def from_others(value):
    size = lax.axis_size("freq")
    return [
        lax.ppermute(value, "freq", [((d + shift) % size, d) for d in range(size)])
        for shift in range(1, size)
    ]


def body(left_basis, right_basis, start_model, recorded, tile_ranks, mute_start, thresholds):
    kept = start_model.shape[0]
    freq_count = kept * lax.axis_size("freq")
    height = start_model.shape[1]
    pieces = pieces_of(height)
    model = [start_model]
    for outer_step in range(OUTER):
        first, last = outer_step == 0, outer_step == OUTER - 1
        outgoing = partials(right_basis, model, tile_ranks, first)
        if first:
            mute, cutoff, ahead, back = tables(mute_start, thresholds, outgoing, kept, freq_count)
        forward = shuffle(outgoing)
        *misfit, outgoing = residual(left_basis, forward, recorded, tile_ranks, last)
        adjoint = shuffle(outgoing)
        spread = []
        for piece, (row, rows) in enumerate(pieces):
            before, before_row = (model[0], row) if first else (model[piece], 0)
            own = update(right_basis, adjoint, before, row, rows, before_row)
            spread.append([own] + from_others(own))
        model = []
        for arrays, (row, rows) in zip(spread, pieces):
            whole_height, earlier = None, []
            if last and row + rows == height:
                whole_height = height
                earlier = [(first_row, value) for (first_row, _), value in zip(pieces, model)]
            model.append(sparsify(arrays, mute, cutoff, ahead, back, row, whole_height, earlier))
    return (model[-1], misfit[0])


def solution(mesh):
    return jax.shard_map(
        body,
        mesh=mesh,
        in_specs=(
            P("freq", "tile", None, None),
            P("freq", "tile", None, None),
            P("freq", "tile", None),
            P("freq", "tile", None),
            P(),
            P("tile", None),
            P(),
        ),
        out_specs=(P("freq", "tile", None), P("freq", "tile", None)),
        check_vma=False,
    )
```
